256 devices in a mesh: req: 32 (over x, z), head: 8 (over y, core).
Axes of the slice: x: 4, y: 4, z: 8, core: 2. Of those that a mesh axis runs over, the one named last changes fastest.
Arguments:
- tokens: bfloat16 [1024, 1280], P(('req', 'head')), may hold values from -6 to 6
- norm_attn: float32 [1280], replicated, may hold values from 0.1 to 1.9
- query_scale: float32 [80], replicated, may hold values from 0.05 to 0.2
- w_query: bfloat16 [1280, 1280], P('head'), may hold values from -0.15625 to 0.15625
- w_key: bfloat16 [1280, 1280], P('head'), may hold values from -0.15625 to 0.15625
- w_value: bfloat16 [1280, 1280], P('head'), may hold values from -0.15625 to 0.15625
- w_out: bfloat16 [1280, 1280], P('head'), may hold values from -0.15625 to 0.15625
- norm_mlp: float32 [1280], replicated, may hold values from 0.1 to 1.9
- w_up: bfloat16 [1280, 1280], P('req'), may hold values from -0.15625 to 0.15625
- w_down: bfloat16 [1280, 1280], P('req'), may hold values from -0.15625 to 0.15625
- cache_k: bfloat16 [1024, 1280, 512], P('req', 'head'), may hold values from -2000 to 2000
- cache_v: bfloat16 [1024, 1280, 512], P('req', 'head'), may hold values from -6 to 6
- lengths: int32 [1024], P('req'), may hold values from 1 to 512, as said below
Outputs:
- layer_out: bfloat16 [1024, 1280], P(('req', 'head'))
The draws below stay inside these ranges and needn't reach their ends.
Inputs may be any that keep to these rules, and one draw needn't show every extreme that they name: `lengths`: each request has this many valid cache slots at the front of its 512; in every draw some request has all 512.
All inputs are finite; a program needn't handle non-finite values.
Results may differ from the reference program's by a relative error of at most 0.012.
The reference program's roundings to bfloat16 on the way (of `normed`, `query`, `new_key`, `probs`, `attended`, `normed_mid` and `hidden`) count: a program that leaves them out, or rounds other values in their place, can miss the bound.
Values may be sent and summed in bfloat16 or wider, within the bound.
A program may use at most 128 MiB of HBM per device.

```python
import math
import jax
import jax.numpy as jnp
from jax import lax

D = 1280
H = 16
HD = 80
F = 1280
CACHE = 512
REQ_DEV = 32
REQ = 1024


def draw_cache_k(key, part):
    base = jnp.clip(jax.random.normal(key, (REQ, H * HD, CACHE), jnp.float32), -6.0, 6.0)
    return base.astype(jnp.bfloat16)


def draw_lengths(key, part):
    first, second, third = jax.random.split(key, 3)
    levels = CACHE.bit_length() - 1
    power = jax.random.randint(first, (REQ,), 0, levels + 1)
    span = jnp.left_shift(jnp.ones((REQ,), jnp.int32), power.astype(jnp.int32))
    extra = jax.random.randint(second, (REQ,), 0, span)
    chosen = jax.random.randint(third, (), 0, REQ)
    lengths = 1 + extra.astype(jnp.int32)
    return jnp.where(jnp.arange(REQ, dtype=jnp.int32) == chosen, CACHE, lengths).astype(jnp.int32)


def shard_levels(stream_key, extent, pieces, low, largest):
    loudness, own = 1.0, jax.random.fold_in(stream_key, 6)
    for axis_at, shards_of in pieces:
        steps = jnp.exp(jax.random.uniform(jax.random.fold_in(own, axis_at), (shards_of,), jnp.float32, low / len(pieces), largest / len(pieces)))
        loudness = loudness * jnp.repeat(steps, extent[axis_at] // shards_of).reshape([-1 if axis == axis_at else 1 for axis in range(len(extent))])
    return loudness


def bell_draw(own_key, shape, scale, limit, cuts=(), kind=jnp.bfloat16):
    level = shard_levels(own_key, shape, cuts, -0.22, 0.18) if cuts else 1.0
    values = jax.random.normal(own_key, shape, jnp.float32) * scale * level
    return jnp.minimum(jnp.maximum(values, -limit), limit).astype(kind)


def setup_inputs(seed: int = 0) -> dict:
    seeds = jax.random.split(jax.random.key(seed), 14)
    return {
        "tokens": bell_draw(seeds[0], (REQ, D), 1.0, 6.0, ((0, 256),)),
        "norm_attn": jnp.clip(1.0 + 0.18 * jax.random.normal(seeds[1], (D,), jnp.float32), 0.1, 1.9),
        "query_scale": jnp.clip(jnp.exp(jax.random.uniform(seeds[2], (HD,), jnp.float32, math.log(0.05), math.log(0.2))), 0.05, 0.2),
        "w_query": bell_draw(seeds[3], (H * HD, D), D ** -0.5, 0.15625, ((0, 8),)),
        "w_key": bell_draw(seeds[4], (H * HD, D), D ** -0.5, 0.15625, ((0, 8),)),
        "w_value": bell_draw(seeds[5], (H * HD, D), D ** -0.5, 0.15625, ((0, 8),)),
        "w_out": bell_draw(seeds[6], (H * HD, D), (H * HD) ** -0.5, 0.15625, ((0, 8),)),
        "norm_mlp": jnp.clip(1.0 + 0.18 * jax.random.normal(seeds[7], (D,), jnp.float32), 0.1, 1.9),
        "w_up": bell_draw(seeds[8], (F, D), D ** -0.5, 0.15625, ((0, 32),)),
        "w_down": bell_draw(seeds[9], (F, D), F ** -0.5, 0.15625, ((0, 32),)),
        "cache_k": draw_cache_k(jax.random.fold_in(seeds[13], 71), 0),
        "cache_v": bell_draw(seeds[11], (REQ, H * HD, CACHE), 1.0, 6.0, ((0, 32), (1, 8))),
        "lengths": draw_lengths(jax.random.fold_in(seeds[13], 71), 0),
    }


def rms_scale(values, gain):
    mean_sq = lax.optimization_barrier(jnp.mean(values * values, axis=-1, keepdims=True))
    return values * lax.rsqrt(mean_sq + 1e-06) * gain

def attend_block(operands):
    query, new_key, new_value, keys, values, lens = operands
    query32 = query.astype(jnp.float32)
    scores = jnp.einsum('rhd,rhdp->rhp', query32, keys.astype(jnp.float32))
    score_new = lax.optimization_barrier(jnp.sum(query32 * new_key.astype(jnp.float32), axis=-1))
    slots = jnp.arange(keys.shape[3], dtype=jnp.int32)
    valid = slots[None, None, :] < lens[:, None, None]
    top = jnp.maximum(lax.optimization_barrier(jnp.max(jnp.where(valid, scores, -jnp.inf), axis=-1)), score_new)
    weights = jnp.where(valid, jnp.exp(scores - top[..., None]), 0.0)
    weight_new = jnp.exp(score_new - top)
    total = lax.optimization_barrier(jnp.sum(weights, axis=-1)) + weight_new
    probs = weights.astype(jnp.bfloat16).astype(jnp.float32)
    prob_new = weight_new.astype(jnp.bfloat16).astype(jnp.float32)
    summed = jnp.einsum('rhp,rhdp->rhd', probs, values.astype(jnp.float32))
    summed = summed + prob_new[..., None] * new_value.astype(jnp.float32)
    result = (summed / total[..., None]).astype(jnp.bfloat16)
    return result.reshape(result.shape[0], -1)

def reference(tokens, norm_attn, query_scale, w_query, w_key, w_value, w_out, norm_mlp, w_up, w_down, cache_k, cache_v, lengths):
    inputs = tokens.astype(jnp.float32)
    normed = rms_scale(inputs, norm_attn).astype(jnp.bfloat16)
    query = jnp.dot(normed, w_query.T, preferred_element_type=jnp.float32).reshape(REQ, H, HD)
    query = (query * query_scale).astype(jnp.bfloat16)
    new_key = jnp.dot(normed, w_key.T, preferred_element_type=jnp.float32).astype(jnp.bfloat16).reshape(REQ, H, HD)
    new_value = jnp.dot(normed, w_value.T, preferred_element_type=jnp.float32).astype(jnp.bfloat16).reshape(REQ, H, HD)
    blocks = REQ // REQ_DEV
    attended = lax.map(attend_block, (query.reshape(blocks, REQ_DEV, H, HD), new_key.reshape(blocks, REQ_DEV, H, HD), new_value.reshape(blocks, REQ_DEV, H, HD), cache_k.reshape(blocks, REQ_DEV, H, HD, CACHE), cache_v.reshape(blocks, REQ_DEV, H, HD, CACHE), lengths.astype(jnp.int32).reshape(blocks, REQ_DEV)))
    attended = attended.reshape(REQ, H * HD)
    mid = inputs + jnp.dot(attended, w_out, preferred_element_type=jnp.float32)
    normed_mid = rms_scale(mid, norm_mlp).astype(jnp.bfloat16)
    hidden = jax.nn.silu(jnp.dot(normed_mid, w_up.T, preferred_element_type=jnp.float32)).astype(jnp.bfloat16)
    return (mid + jnp.dot(hidden, w_down, preferred_element_type=jnp.float32)).astype(jnp.bfloat16)
```

```python
import jax
import jax.numpy as jnp
from jax import lax
from jax.experimental import pallas as pl
from jax.experimental.pallas import tpu as pltpu
from jax.sharding import PartitionSpec as P

MESH = pl.DeviceIdType.MESH
D = 1280
HD = 80
FEATS = 160
ROWS = 32
CACHE = 512
OWN = 4
HEADS = 8
PEERS = 16
UNITS = 40
F32 = jnp.float32
BF16 = jnp.bfloat16


def rms_scale(values, gain):
    mean_sq = jnp.mean(values * values, axis=-1, keepdims=True)
    return values * lax.rsqrt(mean_sq + 1e-06) * gain


def times_rows(left, right):
    return lax.dot_general(left, right, (((1,), (1,)), ((), ())), preferred_element_type=F32)


def times(left, right):
    return lax.dot_general(left, right, (((1,), (0,)), ((), ())), preferred_element_type=F32)


def layer(
    tok_hbm, gain_attn_ref, scale_ref, wq_hbm, wk_hbm, wv_hbm, wo_hbm, gain_mlp_ref, wu_hbm, wd_hbm,
    ck_hbm, cv_hbm, lens_ref, out_ref,
    tok_buf, rows_buf, wq_buf, wk_buf, wv_buf, wo_buf, k_buf, v_buf, wu_buf, wd_buf, spread_buf, att_buf,
    part_send, part_recv, nm_buf, nm_rows, ff_send, ff_recv,
    load_sem, k_sem, v_sem,
    tok_ssem, tok_rsem, part_ssem, part_rsem, nm_ssem, nm_rsem, ff_ssem, ff_rsem, w_ssem, w_rsem,
):
    me_req = lax.axis_index("req")
    me_head = lax.axis_index("head")
    x = me_req // 8
    z = me_req % 8
    y = me_head // 2
    core = me_head % 2
    place = x * 4 + (z % 2) * 2 + core

    def head_peer(k):
        return (me_req, (me_head + k) % HEADS)

    def near_peer(k):
        at = (place + k) % PEERS
        return ((at // 4) * 8 + (z // 2) * 2 + (at // 2) % 2, y * 2 + at % 2)

    def z_peer(k, at_core):
        return (x * 8 + (z + k) % 8, y * 2 + at_core)

    load_tok = pltpu.make_async_copy(tok_hbm, tok_buf.at[me_head], load_sem.at[0])
    load_tok.start()
    loads = []
    for n, (src, dst) in enumerate(((wq_hbm, wq_buf), (wk_hbm, wk_buf), (wv_hbm, wv_buf))):
        loads.append(pltpu.make_async_copy(src, dst, load_sem.at[1 + n]))
        loads[-1].start()
    load_k, load_v = [], []
    for g in range(4):
        rows = pl.ds(g * D, D)
        load_k.append(pltpu.make_async_copy(ck_hbm.at[rows], k_buf.at[rows], k_sem.at[g]))
        load_k[-1].start()
    for g in range(4):
        rows = pl.ds(g * D, D)
        load_v.append(pltpu.make_async_copy(cv_hbm.at[rows], v_buf.at[rows], v_sem.at[g]))
        load_v[-1].start()
    load_wo = pltpu.make_async_copy(wo_hbm, wo_buf, load_sem.at[4])
    load_wo.start()
    load_wu = pltpu.make_async_copy(wu_hbm, wu_buf.at[0], load_sem.at[5])
    load_wd = pltpu.make_async_copy(wd_hbm, wd_buf.at[0], load_sem.at[6])

    barrier = pltpu.get_barrier_semaphore()
    for k in range(1, HEADS):
        pl.semaphore_signal(barrier, inc=1, device_id=head_peer(k), device_id_type=MESH)
    for k in range(1, PEERS):
        pl.semaphore_signal(barrier, inc=1, device_id=near_peer(k), device_id_type=MESH)
    for k in (2, 6):
        pl.semaphore_signal(barrier, inc=1, device_id=z_peer(k, 1 - core), device_id_type=MESH)

    column = lax.broadcasted_iota(jnp.int32, (1, D), 1)
    block = jnp.zeros((1, D), jnp.int32)
    for n in range(1, 8):
        block = block + (column >= n * FEATS).astype(jnp.int32)
    feature = column - block * FEATS
    feature_rows = lax.broadcasted_iota(jnp.int32, (FEATS, D), 0)
    spread_buf[...] = jnp.where(feature_rows == feature, 1.0, 0.0).astype(BF16)
    request = lax.broadcasted_iota(jnp.int32, (8, D), 0)
    masks = (
        (request == block) & (feature < HD),
        (request == block) & (feature >= HD),
    )

    load_tok.wait()
    pl.semaphore_wait(barrier, HEADS - 1 + PEERS - 1 + 2)

    def remote(src, dst, ssem, rsem, device):
        return pltpu.make_async_remote_copy(
            src_ref=src, dst_ref=dst, send_sem=ssem, recv_sem=rsem, device_id=device, device_id_type=MESH
        )

    tok_out = []
    for k in range(1, HEADS):
        copy = remote(
            tok_buf.at[me_head], tok_buf.at[me_head], tok_ssem.at[k], tok_rsem.at[k], head_peer(k)
        )
        copy.start()
        tok_out.append(copy)

    def shard_copies(n, k):
        return (
            remote(wu_hbm, wu_buf.at[n], w_ssem.at[2 * n], w_rsem.at[2 * n], z_peer(k, 1)),
            remote(wd_hbm, wd_buf.at[n], w_ssem.at[2 * n + 1], w_rsem.at[2 * n + 1], z_peer(k, 1)),
        )

    def passed_on():
        return (
            remote(wu_buf.at[0], wu_buf.at[1], w_ssem.at[0], w_rsem.at[2], z_peer(6, 0)),
            remote(wd_buf.at[1], wd_buf.at[1], w_ssem.at[1], w_rsem.at[3], z_peer(2, 0)),
        )

    @pl.when(core == 0)
    def _():
        for n, k in ((0, 6), (1, 2)):
            for copy in shard_copies(n, k):
                copy.start()
        load_wu.start()
        load_wd.start()

    for copy in tok_out:
        copy.wait_recv()
    for n in range(HEADS):
        rows_buf[pl.ds(OWN * n, OWN), :] = tok_buf[n].astype(F32)
    normed = rms_scale(rows_buf[...], gain_attn_ref[...]).astype(BF16)

    for copy in loads:
        copy.wait()
    scale = scale_ref[...]
    scale = jnp.concatenate([scale, scale], axis=1)
    query = (times_rows(normed, wq_buf[...]) * scale).astype(BF16)
    new_key = times_rows(normed, wk_buf[...]).astype(BF16)
    new_value = times_rows(normed, wv_buf[...]).astype(BF16)
    spread_query = times(query, spread_buf[...])
    spread_value = times(new_value, spread_buf[...])
    product = query.astype(F32) * new_key.astype(F32)
    lane = lax.broadcasted_iota(jnp.int32, (ROWS, FEATS), 1)
    score_new = (
        jnp.sum(jnp.where(lane < HD, product, 0.0), axis=-1, keepdims=True),
        jnp.sum(jnp.where(lane >= HD, product, 0.0), axis=-1, keepdims=True),
    )
    eye = lax.broadcasted_iota(jnp.int32, (ROWS, ROWS), 0) == lax.broadcasted_iota(jnp.int32, (ROWS, ROWS), 1)
    lens = jnp.sum(jnp.where(eye, jnp.broadcast_to(lens_ref[...], (ROWS, ROWS)), 0), axis=-1, keepdims=True)

    slot = lax.broadcasted_iota(jnp.int32, (16, CACHE), 1)
    scores = []
    for g in range(4):
        at = slice(8 * g, 8 * g + 8)
        load_k[g].wait()
        left = jnp.concatenate([jnp.where(mask, spread_query[at], 0.0) for mask in masks], axis=0)
        scores.append(times(left.astype(BF16), k_buf[pl.ds(g * D, D), :]))
    probs, prob_new, total = [], [], []
    for g in range(4):
        at = slice(8 * g, 8 * g + 8)
        fresh = jnp.concatenate([score_new[0][at], score_new[1][at]], axis=0)
        length = jnp.concatenate([lens[at], lens[at]], axis=0)
        valid = slot < length
        top = jnp.maximum(jnp.max(jnp.where(valid, scores[g], -jnp.inf), axis=-1, keepdims=True), fresh)
        weights = jnp.where(valid, jnp.exp(scores[g] - top), 0.0)
        weight_new = jnp.exp(fresh - top)
        total.append(jnp.sum(weights, axis=-1, keepdims=True) + weight_new)
        probs.append(weights.astype(BF16))
        prob_new.append(weight_new.astype(BF16).astype(F32))
    for g in range(4):
        at = slice(8 * g, 8 * g + 8)
        load_v[g].wait()
        summed = times_rows(probs[g], v_buf[pl.ds(g * D, D), :])
        picked = jnp.zeros((8, D), F32)
        for h in range(2):
            half = slice(8 * h, 8 * h + 8)
            result = (summed[half] + prob_new[g][half] * spread_value[at]) / total[g][half]
            picked = jnp.where(masks[h], result, picked)
        att_buf[pl.ds(8 * g, 8), :] = picked
    attended = times_rows(att_buf[...].astype(BF16), spread_buf[...]).astype(BF16)
    load_wo.wait()
    part = times(attended, wo_buf[...])
    for n in range(HEADS):
        part_send[n] = part[OWN * n : OWN * n + OWN].astype(BF16)
    part_out = []
    for k in range(1, HEADS):
        copy = remote(
            part_send.at[(me_head + k) % HEADS], part_recv.at[k], part_ssem.at[k], part_rsem.at[k], head_peer(k)
        )
        copy.start()
        part_out.append(copy)

    @pl.when(core == 1)
    def _():
        for n, k in ((0, 6), (1, 2)):
            for copy in shard_copies(n, k):
                copy.wait_recv()
        for copy in passed_on():
            copy.start()

    mid = tok_buf[me_head].astype(F32)
    mid = mid + part_send[me_head].astype(F32)
    for k, copy in enumerate(part_out, start=1):
        copy.wait_recv()
        mid = mid + part_recv[k].astype(F32)
    nm_buf[0] = rms_scale(mid, gain_mlp_ref[...]).astype(BF16)
    nm_out = []
    for k in range(1, PEERS):
        copy = remote(nm_buf.at[0], nm_buf.at[k], nm_ssem.at[k], nm_rsem.at[k], near_peer(k))
        copy.start()
        nm_out.append(copy)

    @pl.when(core == 0)
    def _():
        load_wu.wait()
        load_wd.wait()
        for copy in passed_on():
            copy.wait_recv()

    for copy in nm_out:
        copy.wait_recv()
    for n in range(PEERS):
        nm_rows[pl.ds(OWN * n, OWN), :] = nm_buf[n].astype(F32)
    normed_mid = nm_rows[...].astype(BF16)
    mixed = jnp.zeros((PEERS * OWN, D), F32)
    for n in range(2):
        hidden = times_rows(normed_mid, wu_buf[n])
        hidden = (hidden / (1.0 + jnp.exp(-hidden))).astype(BF16)
        mixed = mixed + times(hidden, wd_buf[n])
    for n in range(PEERS):
        ff_send[n] = mixed[OWN * n : OWN * n + OWN].astype(BF16)
    ff_out = []
    for k in range(1, PEERS):
        copy = remote(ff_send.at[PEERS - k], ff_recv.at[k], ff_ssem.at[k], ff_rsem.at[k], near_peer(k))
        copy.start()
        ff_out.append(copy)
    result = mid + ff_send[0].astype(F32)
    for k, copy in enumerate(ff_out, start=1):
        copy.wait_recv()
        result = result + ff_recv[k].astype(F32)
    out_ref[...] = result.astype(BF16)

    for copy in tok_out + part_out + nm_out + ff_out:
        copy.wait_send()

    @pl.when(core == 0)
    def _():
        for n, k in ((0, 6), (1, 2)):
            for copy in shard_copies(n, k):
                copy.wait_send()

    @pl.when(core == 1)
    def _():
        for copy in passed_on():
            copy.wait_send()


def shards(
    tokens, norm_attn, query_scale, w_query, w_key, w_value, w_out, norm_mlp, w_up, w_down, cache_k, cache_v, lengths
):
    anywhere = pl.BlockSpec(memory_space=pl.ANY)
    vmem = pl.BlockSpec(memory_space=pltpu.VMEM)
    dma = pltpu.SemaphoreType.DMA
    return pl.pallas_call(
        layer,
        out_shape=jax.ShapeDtypeStruct((OWN, D), BF16),
        in_specs=[anywhere, vmem, vmem, anywhere, anywhere, anywhere, anywhere, vmem]
        + [anywhere] * 4 + [vmem],
        out_specs=vmem,
        scratch_shapes=[
            pltpu.VMEM((HEADS, OWN, D), BF16),
            pltpu.VMEM((ROWS, D), F32),
            pltpu.VMEM((FEATS, D), BF16),
            pltpu.VMEM((FEATS, D), BF16),
            pltpu.VMEM((FEATS, D), BF16),
            pltpu.VMEM((FEATS, D), BF16),
            pltpu.VMEM((ROWS * FEATS, CACHE), BF16),
            pltpu.VMEM((ROWS * FEATS, CACHE), BF16),
            pltpu.VMEM((2, UNITS, D), BF16),
            pltpu.VMEM((2, UNITS, D), BF16),
            pltpu.VMEM((FEATS, D), BF16),
            pltpu.VMEM((ROWS, D), F32),
            pltpu.VMEM((HEADS, OWN, D), BF16),
            pltpu.VMEM((HEADS, OWN, D), BF16),
            pltpu.VMEM((PEERS, OWN, D), BF16),
            pltpu.VMEM((PEERS * OWN, D), F32),
            pltpu.VMEM((PEERS, OWN, D), BF16),
            pltpu.VMEM((PEERS, OWN, D), BF16),
            dma((7,)), dma((4,)), dma((4,)),
            dma((HEADS,)), dma((HEADS,)), dma((HEADS,)), dma((HEADS,)),
            dma((PEERS,)), dma((PEERS,)), dma((PEERS,)), dma((PEERS,)),
            dma((4,)), dma((4,)),
        ],
        compiler_params=pltpu.CompilerParams(
            collective_id=0, has_side_effects=True, vmem_limit_bytes=60 * 1024 * 1024
        ),
        name="decode_layer",
    )(
        tokens, norm_attn.reshape(1, D), query_scale.reshape(1, HD), w_query, w_key, w_value, w_out,
        norm_mlp.reshape(1, D), w_up, w_down, cache_k.reshape(ROWS * FEATS, CACHE),
        cache_v.reshape(ROWS * FEATS, CACHE), lengths.reshape(1, ROWS),
    )


def solution(mesh):
    in_specs = (
        P(("req", "head"), None),
        P(),
        P(),
        P("head", None),
        P("head", None),
        P("head", None),
        P("head", None),
        P(),
        P("req", None),
        P("req", None),
        P("req", "head", None),
        P("req", "head", None),
        P("req"),
    )
    out_specs = P(("req", "head"), None)
    return jax.shard_map(shards, mesh=mesh, in_specs=in_specs, out_specs=out_specs, check_vma=False)
```

```python
import jax
import jax.numpy as jnp
from jax import lax
from jax.experimental import pallas as pl
from jax.experimental.pallas import tpu as pltpu
from jax.sharding import PartitionSpec as P

MESH = pl.DeviceIdType.MESH
D = 1280
HD = 80
FEATS = 160
ROWS = 32
CACHE = 512
OWN = 4
HEADS = 8
PEERS = 16
UNITS = 40
F32 = jnp.float32
BF16 = jnp.bfloat16


def rms_scale(values, gain):
    mean_sq = jnp.mean(values * values, axis=-1, keepdims=True)
    return values * lax.rsqrt(mean_sq + 1e-06) * gain


def times_rows(left, right):
    return lax.dot_general(left, right, (((1,), (1,)), ((), ())), preferred_element_type=F32)


def times(left, right):
    return lax.dot_general(left, right, (((1,), (0,)), ((), ())), preferred_element_type=F32)


def layer(
    tok_hbm, gain_attn_hbm, scale_hbm, wq_hbm, wk_hbm, wv_hbm, wo_hbm, gain_mlp_hbm, wu_hbm, wd_hbm,
    ck_hbm, cv_hbm, lens_hbm, out_hbm,
    gain_attn_ref, scale_ref, gain_mlp_ref, lens_ref, out_ref,
    tok_buf, rows_buf, wq_buf, wk_buf, wv_buf, wo_buf, k_buf, v_buf, wu_buf, wd_buf, spread_buf, att_buf,
    part_send, part_recv, nm_buf, nm_rows, ff_send, ff_recv,
    load_sem, small_sem, k_sem, v_sem, ready_sem,
    tok_ssem, tok_rsem, part_ssem, part_rsem, nm_ssem, nm_rsem, ff_ssem, ff_rsem, w_ssem, w_rsem,
):
    me_req = lax.axis_index("req")
    me_head = lax.axis_index("head")
    x = me_req // 8
    z = me_req % 8
    y = me_head // 2
    core = me_head % 2
    place = x * 4 + (z % 2) * 2 + core

    def head_peer(k):
        return (me_req, (me_head + k) % HEADS)

    def near_peer(k):
        at = (place + k) % PEERS
        return ((at // 4) * 8 + (z // 2) * 2 + (at // 2) % 2, y * 2 + at % 2)

    def z_peer(k, at_core):
        return (x * 8 + (z + k) % 8, y * 2 + at_core)

    later = (z < 6, z < 2)
    barrier = pltpu.get_barrier_semaphore()
    for k in range(1, HEADS):
        pl.semaphore_signal(barrier, inc=1, device_id=head_peer(k), device_id_type=MESH)
    for k in range(1, PEERS):
        pl.semaphore_signal(barrier, inc=1, device_id=near_peer(k), device_id_type=MESH)
    for n, k in enumerate((2, 6)):
        @pl.when(later[n])
        def _():
            pl.semaphore_signal(barrier, inc=1, device_id=z_peer(k, 1 - core), device_id_type=MESH)

    load_tok = pltpu.make_async_copy(tok_hbm, tok_buf.at[me_head], load_sem.at[0])
    load_tok.start()
    smalls = []
    for n, (src, dst) in enumerate((
        (gain_attn_hbm, gain_attn_ref), (scale_hbm, scale_ref), (lens_hbm, lens_ref), (gain_mlp_hbm, gain_mlp_ref)
    )):
        smalls.append(pltpu.make_async_copy(src, dst, small_sem.at[n]))
        smalls[-1].start()
    loads = []
    for n, (src, dst) in enumerate(((wq_hbm, wq_buf), (wk_hbm, wk_buf), (wv_hbm, wv_buf))):
        loads.append(pltpu.make_async_copy(src, dst, load_sem.at[1 + n]))
        loads[-1].start()
    load_k, load_v = [], []
    for g in range(4):
        rows = pl.ds(g * D, D)
        load_k.append(pltpu.make_async_copy(ck_hbm.at[rows], k_buf.at[rows], k_sem.at[g]))
        load_k[-1].start()
    for g in range(4):
        rows = pl.ds(g * D, D)
        load_v.append(pltpu.make_async_copy(cv_hbm.at[rows], v_buf.at[rows], v_sem.at[g]))
        load_v[-1].start()
    load_wo = pltpu.make_async_copy(wo_hbm, wo_buf, load_sem.at[4])
    load_wo.start()
    load_wu = pltpu.make_async_copy(wu_hbm, wu_buf.at[0], load_sem.at[5])
    load_wd = pltpu.make_async_copy(wd_hbm, wd_buf.at[0], load_sem.at[6])

    column = lax.broadcasted_iota(jnp.int32, (1, D), 1)
    block = jnp.zeros((1, D), jnp.int32)
    for n in range(1, 8):
        block = block + (column >= n * FEATS).astype(jnp.int32)
    feature = column - block * FEATS
    feature_rows = lax.broadcasted_iota(jnp.int32, (FEATS, D), 0)
    spread_buf[...] = jnp.where(feature_rows == feature, 1.0, 0.0).astype(BF16)
    request = lax.broadcasted_iota(jnp.int32, (8, D), 0)
    masks = (
        (request == block) & (feature < HD),
        (request == block) & (feature >= HD),
    )

    load_tok.wait()
    pl.semaphore_wait(barrier, HEADS - 1 + PEERS - 1 + (z >= 2).astype(jnp.int32) + (z >= 6).astype(jnp.int32))

    def remote(src, dst, ssem, rsem, device):
        return pltpu.make_async_remote_copy(
            src_ref=src, dst_ref=dst, send_sem=ssem, recv_sem=rsem, device_id=device, device_id_type=MESH
        )

    tok_out = []
    for k in range(1, HEADS):
        copy = remote(
            tok_buf.at[me_head], tok_buf.at[me_head], tok_ssem.at[k], tok_rsem.at[k], head_peer(k)
        )
        copy.start()
        tok_out.append(copy)

    def shard_copies(n, k):
        return (
            remote(wu_hbm, wu_buf.at[n], w_ssem.at[2 * n], w_rsem.at[2 * n], z_peer(k, 1)),
            remote(wd_hbm, wd_buf.at[n], w_ssem.at[2 * n + 1], w_rsem.at[2 * n + 1], z_peer(k, 1)),
        )

    def passed_on():
        return (
            remote(wu_buf.at[0], wu_buf.at[1], w_ssem.at[0], w_rsem.at[2], z_peer(6, 0)),
            remote(wd_buf.at[1], wd_buf.at[1], w_ssem.at[1], w_rsem.at[3], z_peer(2, 0)),
        )

    for n, k in enumerate((2, 6)):
        @pl.when(jnp.logical_not(later[n]))
        def _():
            pl.semaphore_signal(ready_sem.at[1 - n], inc=1, device_id=z_peer(k, 1 - core), device_id_type=MESH)

            @pl.when(core == 0)
            def _():
                for copy in shard_copies(1 - n, k):
                    copy.start()

    def send_later(n, k):
        @pl.when(later[n])
        def _():
            pl.semaphore_wait(ready_sem.at[n], 1)

            @pl.when(core == 0)
            def _():
                for copy in shard_copies(1 - n, k):
                    copy.start()

    @pl.when(core == 0)
    def _():
        load_wu.start()
        load_wd.start()

    for copy in tok_out:
        copy.wait_recv()
    for n in range(HEADS):
        rows_buf[pl.ds(OWN * n, OWN), :] = tok_buf[n].astype(F32)
    for copy in smalls:
        copy.wait()
    normed = rms_scale(rows_buf[...], gain_attn_ref[...].reshape(1, D)).astype(BF16)

    for copy in loads:
        copy.wait()
    scale = scale_ref[...]
    scale = jnp.concatenate([scale, scale], axis=1)
    query = (times_rows(normed, wq_buf[...]) * scale).astype(BF16)
    new_key = times_rows(normed, wk_buf[...]).astype(BF16)
    new_value = times_rows(normed, wv_buf[...]).astype(BF16)
    spread_query = times(query, spread_buf[...])
    spread_value = times(new_value, spread_buf[...])
    product = query.astype(F32) * new_key.astype(F32)
    lane = lax.broadcasted_iota(jnp.int32, (ROWS, FEATS), 1)
    score_new = (
        jnp.sum(jnp.where(lane < HD, product, 0.0), axis=-1, keepdims=True),
        jnp.sum(jnp.where(lane >= HD, product, 0.0), axis=-1, keepdims=True),
    )
    eye = lax.broadcasted_iota(jnp.int32, (ROWS, ROWS), 0) == lax.broadcasted_iota(jnp.int32, (ROWS, ROWS), 1)
    lens = jnp.sum(jnp.where(eye, jnp.broadcast_to(lens_ref[...], (ROWS, ROWS)), 0), axis=-1, keepdims=True)

    send_later(0, 2)
    slot = lax.broadcasted_iota(jnp.int32, (16, CACHE), 1)
    scores = []
    for g in range(4):
        at = slice(8 * g, 8 * g + 8)
        load_k[g].wait()
        left = jnp.concatenate([jnp.where(mask, spread_query[at], 0.0) for mask in masks], axis=0)
        scores.append(times(left.astype(BF16), k_buf[pl.ds(g * D, D), :]))
    probs, prob_new, total = [], [], []
    for g in range(4):
        at = slice(8 * g, 8 * g + 8)
        fresh = jnp.concatenate([score_new[0][at], score_new[1][at]], axis=0)
        length = jnp.concatenate([lens[at], lens[at]], axis=0)
        valid = slot < length
        top = jnp.maximum(jnp.max(jnp.where(valid, scores[g], -jnp.inf), axis=-1, keepdims=True), fresh)
        weights = jnp.where(valid, jnp.exp(scores[g] - top), 0.0)
        weight_new = jnp.exp(fresh - top)
        total.append(jnp.sum(weights, axis=-1, keepdims=True) + weight_new)
        probs.append(weights.astype(BF16))
        prob_new.append(weight_new.astype(BF16).astype(F32))
    for g in range(4):
        at = slice(8 * g, 8 * g + 8)
        load_v[g].wait()
        summed = times_rows(probs[g], v_buf[pl.ds(g * D, D), :])
        picked = jnp.zeros((8, D), F32)
        for h in range(2):
            half = slice(8 * h, 8 * h + 8)
            result = (summed[half] + prob_new[g][half] * spread_value[at]) / total[g][half]
            picked = jnp.where(masks[h], result, picked)
        att_buf[pl.ds(8 * g, 8), :] = picked
    attended = times_rows(att_buf[...].astype(BF16), spread_buf[...]).astype(BF16)
    load_wo.wait()
    part = times(attended, wo_buf[...])
    for n in range(HEADS):
        part_send[n] = part[OWN * n : OWN * n + OWN].astype(BF16)
    part_out = []
    for k in range(1, HEADS):
        copy = remote(
            part_send.at[(me_head + k) % HEADS], part_recv.at[k], part_ssem.at[k], part_rsem.at[k], head_peer(k)
        )
        copy.start()
        part_out.append(copy)

    send_later(1, 6)

    @pl.when(core == 1)
    def _():
        for n, k in ((0, 6), (1, 2)):
            for copy in shard_copies(n, k):
                copy.wait_recv()
        for copy in passed_on():
            copy.start()

    mid = tok_buf[me_head].astype(F32)
    mid = mid + part_send[me_head].astype(F32)
    for k, copy in enumerate(part_out, start=1):
        copy.wait_recv()
        mid = mid + part_recv[k].astype(F32)
    nm_buf[0] = rms_scale(mid, gain_mlp_ref[...].reshape(1, D)).astype(BF16)
    nm_out = []
    for k in range(1, PEERS):
        copy = remote(nm_buf.at[0], nm_buf.at[k], nm_ssem.at[k], nm_rsem.at[k], near_peer(k))
        copy.start()
        nm_out.append(copy)

    @pl.when(core == 0)
    def _():
        load_wu.wait()
        load_wd.wait()
        for copy in passed_on():
            copy.wait_recv()

    for copy in nm_out:
        copy.wait_recv()
    for n in range(PEERS):
        nm_rows[pl.ds(OWN * n, OWN), :] = nm_buf[n].astype(F32)
    normed_mid = nm_rows[...].astype(BF16)
    mixed = jnp.zeros((PEERS * OWN, D), F32)
    for n in range(2):
        hidden = times_rows(normed_mid, wu_buf[n])
        hidden = (hidden / (1.0 + jnp.exp(-hidden))).astype(BF16)
        mixed = mixed + times(hidden, wd_buf[n])
    for n in range(PEERS):
        ff_send[n] = mixed[OWN * n : OWN * n + OWN].astype(BF16)
    ff_out = []
    for k in range(1, PEERS):
        copy = remote(ff_send.at[PEERS - k], ff_recv.at[k], ff_ssem.at[k], ff_rsem.at[k], near_peer(k))
        copy.start()
        ff_out.append(copy)
    result = mid + ff_send[0].astype(F32)
    for k, copy in enumerate(ff_out, start=1):
        copy.wait_recv()
        result = result + ff_recv[k].astype(F32)
    out_ref[...] = result.astype(BF16)
    store_out = pltpu.make_async_copy(out_ref, out_hbm, load_sem.at[7])
    store_out.start()

    for copy in tok_out + part_out + nm_out + ff_out:
        copy.wait_send()

    @pl.when(core == 0)
    def _():
        for n, k in ((0, 6), (1, 2)):
            for copy in shard_copies(n, k):
                copy.wait_send()

    @pl.when(core == 1)
    def _():
        for copy in passed_on():
            copy.wait_send()

    store_out.wait()


def shards(
    tokens, norm_attn, query_scale, w_query, w_key, w_value, w_out, norm_mlp, w_up, w_down, cache_k, cache_v, lengths
):
    anywhere = pl.BlockSpec(memory_space=pl.ANY)
    dma = pltpu.SemaphoreType.DMA
    return pl.pallas_call(
        layer,
        out_shape=jax.ShapeDtypeStruct((OWN, D), BF16),
        in_specs=[anywhere] * 13,
        out_specs=anywhere,
        scratch_shapes=[
            pltpu.VMEM((D,), F32),
            pltpu.VMEM((1, HD), F32),
            pltpu.VMEM((D,), F32),
            pltpu.VMEM((1, ROWS), jnp.int32),
            pltpu.VMEM((OWN, D), BF16),
            pltpu.VMEM((HEADS, OWN, D), BF16),
            pltpu.VMEM((ROWS, D), F32),
            pltpu.VMEM((FEATS, D), BF16),
            pltpu.VMEM((FEATS, D), BF16),
            pltpu.VMEM((FEATS, D), BF16),
            pltpu.VMEM((FEATS, D), BF16),
            pltpu.VMEM((ROWS * FEATS, CACHE), BF16),
            pltpu.VMEM((ROWS * FEATS, CACHE), BF16),
            pltpu.VMEM((2, UNITS, D), BF16),
            pltpu.VMEM((2, UNITS, D), BF16),
            pltpu.VMEM((FEATS, D), BF16),
            pltpu.VMEM((ROWS, D), F32),
            pltpu.VMEM((HEADS, OWN, D), BF16),
            pltpu.VMEM((HEADS, OWN, D), BF16),
            pltpu.VMEM((PEERS, OWN, D), BF16),
            pltpu.VMEM((PEERS * OWN, D), F32),
            pltpu.VMEM((PEERS, OWN, D), BF16),
            pltpu.VMEM((PEERS, OWN, D), BF16),
            dma((8,)), dma((4,)), dma((4,)), dma((4,)), pltpu.SemaphoreType.REGULAR((2,)),
            dma((HEADS,)), dma((HEADS,)), dma((HEADS,)), dma((HEADS,)),
            dma((PEERS,)), dma((PEERS,)), dma((PEERS,)), dma((PEERS,)),
            dma((4,)), dma((4,)),
        ],
        compiler_params=pltpu.CompilerParams(
            collective_id=0, has_side_effects=True, vmem_limit_bytes=60 * 1024 * 1024
        ),
        name="decode_layer",
    )(
        tokens, norm_attn, query_scale.reshape(1, HD), w_query, w_key, w_value, w_out,
        norm_mlp, w_up, w_down, cache_k.reshape(ROWS * FEATS, CACHE),
        cache_v.reshape(ROWS * FEATS, CACHE), lengths.reshape(1, ROWS),
    )


def solution(mesh):
    in_specs = (
        P(("req", "head"), None),
        P(),
        P(),
        P("head", None),
        P("head", None),
        P("head", None),
        P("head", None),
        P(),
        P("req", None),
        P("req", None),
        P("req", "head", None),
        P("req", "head", None),
        P("req"),
    )
    out_specs = P(("req", "head"), None)
    return jax.shard_map(shards, mesh=mesh, in_specs=in_specs, out_specs=out_specs, check_vma=False)
```

```python
import jax
import jax.numpy as jnp
from jax import lax
from jax.experimental import pallas as pl
from jax.experimental.pallas import tpu as pltpu
from jax.sharding import PartitionSpec as P

MESH = pl.DeviceIdType.MESH
D = 1280
HD = 80
FEATS = 160
ROWS = 32
CACHE = 512
OWN = 4
HEADS = 8
PEERS = 8
UNITS = 40
SHARDS = 4
F32 = jnp.float32
BF16 = jnp.bfloat16


def rms_scale(values, gain):
    mean_sq = jnp.mean(values * values, axis=-1, keepdims=True)
    return values * lax.rsqrt(mean_sq + 1e-06) * gain


def times_rows(left, right):
    return lax.dot_general(left, right, (((1,), (1,)), ((), ())), preferred_element_type=F32)


def times(left, right):
    return lax.dot_general(left, right, (((1,), (0,)), ((), ())), preferred_element_type=F32)


def layer(
    tok_hbm, gain_attn_hbm, scale_hbm, wq_hbm, wk_hbm, wv_hbm, wo_hbm, gain_mlp_hbm, wu_hbm, wd_hbm,
    ck_hbm, cv_hbm, lens_hbm, out_ref,
    gain_attn_ref, scale_ref, gain_mlp_ref, lens_ref,
    tok_buf, rows_buf, wq_buf, wk_buf, wv_buf, wo_buf, k_buf, v_buf, wu_buf, wd_buf, spread_buf, att_buf,
    part_send, part_recv, nm_buf, nm_rows, ff_send, ff_recv,
    load_sem, small_sem, k_sem, v_sem, ready_sem,
    tok_ssem, tok_rsem, part_ssem, part_rsem, nm_ssem, nm_rsem, ff_ssem, ff_rsem, wu_ssem, wu_rsem, wd_ssem, wd_rsem,
):
    me_req = lax.axis_index("req")
    me_head = lax.axis_index("head")
    x = me_req // 8
    z = me_req % 8
    y = me_head // 2
    core = me_head % 2
    place = x * 2 + core

    def head_peer(k):
        return (me_req, (me_head + k) % HEADS)

    def near_peer(k):
        at = (place + k) % PEERS
        return ((at // 2) * 8 + z, y * 2 + at % 2)

    away = 2 - core

    def z_peer(n):
        at_z = (z + (away, 8 - away, 1, 7)[n]) % 8
        at_core = core if n < 2 else 1 - core
        return (x * 8 + at_z, y * 2 + at_core), at_z

    def start(at_z):
        return jnp.minimum(at_z, 4)

    later = [start(z_peer(n)[1]) > start(z) for n in range(4)]
    earlier = [start(z_peer(n)[1]) < start(z) for n in range(4)]
    expected = HEADS - 1 + PEERS - 1
    for n in range(4):
        expected = expected + 1 - later[n].astype(jnp.int32)
    barrier = pltpu.get_barrier_semaphore()
    for k in range(1, HEADS):
        pl.semaphore_signal(barrier, inc=1, device_id=head_peer(k), device_id_type=MESH)
    for k in range(1, PEERS):
        pl.semaphore_signal(barrier, inc=1, device_id=near_peer(k), device_id_type=MESH)
    for n in range(4):
        @pl.when(jnp.logical_not(earlier[n]))
        def _():
            pl.semaphore_signal(barrier, inc=1, device_id=z_peer(n)[0], device_id_type=MESH)

    load_tok = pltpu.make_async_copy(tok_hbm, tok_buf.at[me_head], load_sem.at[0])
    load_tok.start()
    smalls = []
    for n, (src, dst) in enumerate((
        (gain_attn_hbm, gain_attn_ref), (scale_hbm, scale_ref), (lens_hbm, lens_ref), (gain_mlp_hbm, gain_mlp_ref)
    )):
        smalls.append(pltpu.make_async_copy(src, dst, small_sem.at[n]))
        smalls[-1].start()
    loads = []
    for n, (src, dst) in enumerate(((wq_hbm, wq_buf), (wk_hbm, wk_buf), (wv_hbm, wv_buf))):
        loads.append(pltpu.make_async_copy(src, dst, load_sem.at[1 + n]))
        loads[-1].start()
    load_k, load_v = [], []
    for g in range(4):
        rows = pl.ds(g * D, D)
        load_k.append(pltpu.make_async_copy(ck_hbm.at[rows], k_buf.at[rows], k_sem.at[g]))
        load_k[-1].start()
    for g in range(4):
        rows = pl.ds(g * D, D)
        load_v.append(pltpu.make_async_copy(cv_hbm.at[rows], v_buf.at[rows], v_sem.at[g]))
        load_v[-1].start()
    load_wo = pltpu.make_async_copy(wo_hbm, wo_buf, load_sem.at[4])
    load_wo.start()
    load_wu = pltpu.make_async_copy(wu_hbm, wu_buf.at[0], load_sem.at[5])
    load_wd = pltpu.make_async_copy(wd_hbm, wd_buf.at[0], load_sem.at[6])

    column = lax.broadcasted_iota(jnp.int32, (1, D), 1)
    block = jnp.zeros((1, D), jnp.int32)
    for n in range(1, 8):
        block = block + (column >= n * FEATS).astype(jnp.int32)
    feature = column - block * FEATS
    feature_rows = lax.broadcasted_iota(jnp.int32, (FEATS, D), 0)
    spread_buf[...] = jnp.where(feature_rows == feature, 1.0, 0.0).astype(BF16)
    request = lax.broadcasted_iota(jnp.int32, (8, D), 0)
    masks = (
        (request == block) & (feature < HD),
        (request == block) & (feature >= HD),
    )

    load_tok.wait()
    pl.semaphore_wait(barrier, expected)

    def remote(src, dst, ssem, rsem, device):
        return pltpu.make_async_remote_copy(
            src_ref=src, dst_ref=dst, send_sem=ssem, recv_sem=rsem, device_id=device, device_id_type=MESH
        )

    tok_out = []
    for k in range(1, HEADS):
        copy = remote(
            tok_buf.at[me_head], tok_buf.at[me_head], tok_ssem.at[k], tok_rsem.at[k], head_peer(k)
        )
        copy.start()
        tok_out.append(copy)

    def own_shard(n):
        slot = 2 - n - core
        device = z_peer(n)[0]
        return (
            remote(wu_hbm, wu_buf.at[slot], wu_ssem.at[n], wu_rsem.at[1 - n], device),
            remote(wd_hbm, wd_buf.at[slot], wd_ssem.at[n], wd_rsem.at[1 - n], device),
        )

    def passed_on(n):
        four, three = z_peer(1 - n)[0], z_peer(3 - n)[0]
        up = remote(wu_buf.at[1 + n], wu_buf.at[2 + n], wu_ssem.at[2 + n], wu_rsem.at[2 + n], three)
        down = remote(wd_buf.at[1 + n], wd_buf.at[2 + n], wd_ssem.at[2 + n], wd_rsem.at[2 + n], three)
        if n == 0:
            far = remote(wu_buf.at[1], wu_buf.at[3], wu_ssem.at[4], wu_rsem.at[2], four)
        else:
            far = remote(wd_buf.at[2], wd_buf.at[3], wd_ssem.at[4], wd_rsem.at[2], four)
        return far, up, down

    for n in range(4):
        @pl.when(earlier[n])
        def _():
            pl.semaphore_signal(ready_sem.at[n + 1 - 2 * (n % 2)], inc=1, device_id=z_peer(n)[0], device_id_type=MESH)

    for n in range(2):
        @pl.when(jnp.logical_not(later[n]))
        def _():
            for copy in own_shard(n):
                copy.start()

    @pl.when(core == 0)
    def _():
        load_wu.start()
        load_wd.start()

    for copy in tok_out:
        copy.wait_recv()
    for n in range(2):
        @pl.when(later[n])
        def _():
            pl.semaphore_wait(ready_sem.at[n], 1)
            for copy in own_shard(n):
                copy.start()

    for n in range(HEADS):
        rows_buf[pl.ds(OWN * n, OWN), :] = tok_buf[n].astype(F32)
    for copy in smalls:
        copy.wait()
    normed = rms_scale(rows_buf[...], gain_attn_ref[...].reshape(1, D)).astype(BF16)

    for copy in loads:
        copy.wait()
    scale = scale_ref[...]
    scale = jnp.concatenate([scale, scale], axis=1)
    query = (times_rows(normed, wq_buf[...]) * scale).astype(BF16)
    new_key = times_rows(normed, wk_buf[...]).astype(BF16)
    new_value = times_rows(normed, wv_buf[...]).astype(BF16)
    spread_query = times(query, spread_buf[...])
    spread_value = times(new_value, spread_buf[...])
    product = query.astype(F32) * new_key.astype(F32)
    lane = lax.broadcasted_iota(jnp.int32, (ROWS, FEATS), 1)
    score_new = (
        jnp.sum(jnp.where(lane < HD, product, 0.0), axis=-1, keepdims=True),
        jnp.sum(jnp.where(lane >= HD, product, 0.0), axis=-1, keepdims=True),
    )
    eye = lax.broadcasted_iota(jnp.int32, (ROWS, ROWS), 0) == lax.broadcasted_iota(jnp.int32, (ROWS, ROWS), 1)
    lens = jnp.sum(jnp.where(eye, jnp.broadcast_to(lens_ref[...], (ROWS, ROWS)), 0), axis=-1, keepdims=True)

    slot = lax.broadcasted_iota(jnp.int32, (16, CACHE), 1)
    scores = []
    for g in range(4):
        at = slice(8 * g, 8 * g + 8)
        load_k[g].wait()
        left = jnp.concatenate([jnp.where(mask, spread_query[at], 0.0) for mask in masks], axis=0)
        scores.append(times(left.astype(BF16), k_buf[pl.ds(g * D, D), :]))
    probs, prob_new, total = [], [], []
    for g in range(4):
        at = slice(8 * g, 8 * g + 8)
        fresh = jnp.concatenate([score_new[0][at], score_new[1][at]], axis=0)
        length = jnp.concatenate([lens[at], lens[at]], axis=0)
        valid = slot < length
        top = jnp.maximum(jnp.max(jnp.where(valid, scores[g], -jnp.inf), axis=-1, keepdims=True), fresh)
        weights = jnp.where(valid, jnp.exp(scores[g] - top), 0.0)
        weight_new = jnp.exp(fresh - top)
        total.append(jnp.sum(weights, axis=-1, keepdims=True) + weight_new)
        probs.append(weights.astype(BF16))
        prob_new.append(weight_new.astype(BF16).astype(F32))
    for g in range(4):
        at = slice(8 * g, 8 * g + 8)
        load_v[g].wait()
        summed = times_rows(probs[g], v_buf[pl.ds(g * D, D), :])
        picked = jnp.zeros((8, D), F32)
        for h in range(2):
            half = slice(8 * h, 8 * h + 8)
            result = (summed[half] + prob_new[g][half] * spread_value[at]) / total[g][half]
            picked = jnp.where(masks[h], result, picked)
        att_buf[pl.ds(8 * g, 8), :] = picked
    attended = times_rows(att_buf[...].astype(BF16), spread_buf[...]).astype(BF16)
    load_wo.wait()
    part = times(attended, wo_buf[...])
    for n in range(HEADS):
        part_send[n] = part[OWN * n : OWN * n + OWN].astype(BF16)
    part_out = []
    for k in range(1, HEADS):
        copy = remote(
            part_send.at[(me_head + k) % HEADS], part_recv.at[k], part_ssem.at[k], part_rsem.at[k], head_peer(k)
        )
        copy.start()
        part_out.append(copy)

    for n in range(2, 4):
        @pl.when(later[n])
        def _():
            pl.semaphore_wait(ready_sem.at[n], 1)

    @pl.when(core == 0)
    def _():
        for n in range(2):
            for copy in own_shard(1 - n):
                copy.wait_recv()
            for copy in passed_on(n):
                copy.start()

    mid = tok_buf[me_head].astype(F32)
    mid = mid + part_send[me_head].astype(F32)
    for k, copy in enumerate(part_out, start=1):
        copy.wait_recv()
        mid = mid + part_recv[k].astype(F32)
    nm_buf[0] = rms_scale(mid, gain_mlp_ref[...].reshape(1, D)).astype(BF16)
    nm_out = []
    for k in range(1, PEERS):
        copy = remote(nm_buf.at[0], nm_buf.at[k], nm_ssem.at[k], nm_rsem.at[k], near_peer(k))
        copy.start()
        nm_out.append(copy)

    @pl.when(core == 0)
    def _():
        load_wu.wait()
        load_wd.wait()
        for n in range(2):
            passed_on(n)[0].wait_recv()

    @pl.when(core == 1)
    def _():
        for n in range(2):
            for copy in own_shard(n) + passed_on(n)[1:]:
                copy.wait_recv()

    for copy in nm_out:
        copy.wait_recv()
    for n in range(PEERS):
        nm_rows[pl.ds(OWN * n, OWN), :] = nm_buf[n].astype(F32)
    normed_mid = nm_rows[...].astype(BF16)
    hidden = times_rows(normed_mid, wu_buf[...].reshape(SHARDS * UNITS, D))
    hidden = (hidden / (1.0 + jnp.exp(-hidden))).astype(BF16)
    mixed = times(hidden, wd_buf[...].reshape(SHARDS * UNITS, D))
    for n in range(PEERS):
        ff_send[n] = mixed[OWN * n : OWN * n + OWN].astype(BF16)
    ff_out = []
    for k in range(1, PEERS):
        copy = remote(ff_send.at[PEERS - k], ff_recv.at[k], ff_ssem.at[k], ff_rsem.at[k], near_peer(k))
        copy.start()
        ff_out.append(copy)
    result = mid + ff_send[0].astype(F32)
    for k, copy in enumerate(ff_out, start=1):
        copy.wait_recv()
        result = result + ff_recv[k].astype(F32)
    out_ref[...] = result.astype(BF16)

    for copy in tok_out + part_out + nm_out + ff_out:
        copy.wait_send()

    for n in range(2):
        for copy in own_shard(n):
            copy.wait_send()

    @pl.when(core == 0)
    def _():
        for n in range(2):
            for copy in passed_on(n):
                copy.wait_send()


def shards(
    tokens, norm_attn, query_scale, w_query, w_key, w_value, w_out, norm_mlp, w_up, w_down, cache_k, cache_v, lengths
):
    anywhere = pl.BlockSpec(memory_space=pl.ANY)
    dma = pltpu.SemaphoreType.DMA
    return pl.pallas_call(
        layer,
        out_shape=pltpu.VMEM((OWN, D), BF16),
        in_specs=[anywhere] * 13,
        out_specs=pl.BlockSpec(memory_space=pltpu.VMEM),
        scratch_shapes=[
            pltpu.VMEM((D,), F32),
            pltpu.VMEM((1, HD), F32),
            pltpu.VMEM((D,), F32),
            pltpu.VMEM((1, ROWS), jnp.int32),
            pltpu.VMEM((HEADS, OWN, D), BF16),
            pltpu.VMEM((ROWS, D), F32),
            pltpu.VMEM((FEATS, D), BF16),
            pltpu.VMEM((FEATS, D), BF16),
            pltpu.VMEM((FEATS, D), BF16),
            pltpu.VMEM((FEATS, D), BF16),
            pltpu.VMEM((ROWS * FEATS, CACHE), BF16),
            pltpu.VMEM((ROWS * FEATS, CACHE), BF16),
            pltpu.VMEM((SHARDS, UNITS, D), BF16),
            pltpu.VMEM((SHARDS, UNITS, D), BF16),
            pltpu.VMEM((FEATS, D), BF16),
            pltpu.VMEM((ROWS, D), F32),
            pltpu.VMEM((HEADS, OWN, D), BF16),
            pltpu.VMEM((HEADS, OWN, D), BF16),
            pltpu.VMEM((PEERS, OWN, D), BF16),
            pltpu.VMEM((PEERS * OWN, D), F32),
            pltpu.VMEM((PEERS, OWN, D), BF16),
            pltpu.VMEM((PEERS, OWN, D), BF16),
            dma((7,)), dma((4,)), dma((4,)), dma((4,)), pltpu.SemaphoreType.REGULAR((4,)),
            dma((HEADS,)), dma((HEADS,)), dma((HEADS,)), dma((HEADS,)),
            dma((PEERS,)), dma((PEERS,)), dma((PEERS,)), dma((PEERS,)),
            dma((5,)), dma((4,)), dma((5,)), dma((4,)),
        ],
        compiler_params=pltpu.CompilerParams(
            collective_id=0, has_side_effects=True, vmem_limit_bytes=60 * 1024 * 1024
        ),
        name="decode_layer",
    )(
        tokens, norm_attn, query_scale.reshape(1, HD), w_query, w_key, w_value, w_out,
        norm_mlp, w_up, w_down, cache_k.reshape(ROWS * FEATS, CACHE),
        cache_v.reshape(ROWS * FEATS, CACHE), lengths.reshape(1, ROWS),
    )


def solution(mesh):
    in_specs = (
        P(("req", "head"), None),
        P(),
        P(),
        P("head", None),
        P("head", None),
        P("head", None),
        P("head", None),
        P(),
        P("req", None),
        P("req", None),
        P("req", "head", None),
        P("req", "head", None),
        P("req"),
    )
    out_specs = P(("req", "head"), None)
    return jax.shard_map(shards, mesh=mesh, in_specs=in_specs, out_specs=out_specs, check_vma=False)
```

```python
import jax
import jax.numpy as jnp
from jax import lax
from jax.experimental import pallas as pl
from jax.experimental.pallas import tpu as pltpu
from jax.sharding import PartitionSpec as P

MESH = pl.DeviceIdType.MESH
D = 1280
HD = 80
FEATS = 160
ROWS = 32
CACHE = 512
OWN = 4
HEADS = 8
PEERS = 8
UNITS = 40
SHARDS = 4
F32 = jnp.float32
BF16 = jnp.bfloat16


def rms_scale(values, gain):
    mean_sq = jnp.mean(values * values, axis=-1, keepdims=True)
    return values * lax.rsqrt(mean_sq + 1e-06) * gain


def times_rows(left, right):
    return lax.dot_general(left, right, (((1,), (1,)), ((), ())), preferred_element_type=F32)


def times(left, right):
    return lax.dot_general(left, right, (((1,), (0,)), ((), ())), preferred_element_type=F32)


def layer(
    tok_hbm, gain_attn_hbm, scale_hbm, wq_hbm, wk_hbm, wv_hbm, wo_hbm, gain_mlp_hbm, wu_hbm, wd_hbm,
    ck_hbm, cv_hbm, lens_hbm, out_ref,
    gain_attn_ref, scale_ref, gain_mlp_ref, lens_ref,
    tok_buf, rows_buf, wq_buf, wk_buf, wv_buf, wo_buf, k_buf, v_buf, w_buf, spread_buf, att_buf,
    part_send, part_recv, nm_buf, nm_rows, ff_send, ff_recv,
    load_sem, small_sem, k_sem, v_sem, ready_sem,
    tok_ssem, tok_rsem, part_ssem, part_rsem, nm_ssem, nm_rsem, ff_ssem, ff_rsem, w_ssem, w_rsem, pair_ssem, pair_rsem,
):
    me_req = lax.axis_index("req")
    me_head = lax.axis_index("head")
    x = lax.div(me_req, 8)
    z = lax.rem(me_req, 8)
    core = lax.rem(me_head, 2)
    z_odd = lax.rem(z, 2)
    z_twin = z + 1 - 2 * z_odd

    def head_peer(k):
        return (me_req, lax.rem(me_head + k, HEADS))

    def near_peer(k):
        return (lax.rem(x + k % 4, 4) * 8 + (z if k < 4 else z_twin), me_head)

    def near_back(k):
        return (4 - k) % 4 + 4 * (k // 4)

    away = (2 + 4 * core, 6 - 4 * core)

    def z_peer(n):
        return (x * 8 + lax.rem(z + away[n], 8), me_head)

    other_core = (me_req, me_head + 1 - 2 * core)

    def start(at_z):
        return jnp.minimum(at_z, 4)

    later = [start(lax.rem(z + away[n], 8)) > start(z) for n in range(2)]
    earlier = [start(lax.rem(z + away[n], 8)) < start(z) for n in range(2)]
    twin_later = start(z_twin) > start(z)
    twin_earlier = start(z_twin) < start(z)
    load_tok = pltpu.make_async_copy(tok_hbm, tok_buf.at[me_head], load_sem.at[0])
    load_tok.start()
    barrier = pltpu.get_barrier_semaphore()
    for k in range(1, HEADS):
        pl.semaphore_signal(barrier, inc=1, device_id=head_peer(k), device_id_type=MESH)
    for k in range(1, 4):
        pl.semaphore_signal(barrier, inc=1, device_id=near_peer(k), device_id_type=MESH)
    expected = HEADS - 1 + 3
    for n in range(2):
        expected = expected + 1 - later[n].astype(jnp.int32)

        @pl.when(jnp.logical_not(earlier[n]))
        def _():
            pl.semaphore_signal(barrier, inc=1, device_id=z_peer(n), device_id_type=MESH)

    expected = expected + 4 - 4 * twin_later.astype(jnp.int32)

    @pl.when(jnp.logical_not(twin_earlier))
    def _():
        for k in range(4, PEERS):
            pl.semaphore_signal(barrier, inc=1, device_id=near_peer(k), device_id_type=MESH)

    smalls = []
    for n, (src, dst) in enumerate((
        (gain_attn_hbm, gain_attn_ref), (scale_hbm, scale_ref), (lens_hbm, lens_ref), (gain_mlp_hbm, gain_mlp_ref)
    )):
        smalls.append(pltpu.make_async_copy(src, dst, small_sem.at[n]))
        smalls[-1].start()
    loads = []
    for n, (src, dst) in enumerate(((wq_hbm, wq_buf), (wk_hbm, wk_buf), (wv_hbm, wv_buf))):
        loads.append(pltpu.make_async_copy(src, dst, load_sem.at[1 + n]))
        loads[-1].start()
    load_k, load_v = [], []
    load_wu = pltpu.make_async_copy(wu_hbm, w_buf.at[0, 0], load_sem.at[5])
    load_wu.start()
    load_wd = pltpu.make_async_copy(wd_hbm, w_buf.at[1, 0], load_sem.at[6])
    load_wd.start()
    for g in range(4):
        rows = pl.ds(g * D, D)
        load_k.append(pltpu.make_async_copy(ck_hbm.at[rows], k_buf.at[rows], k_sem.at[g]))
        load_k[-1].start()
    for g in range(4):
        rows = pl.ds(g * D, D)
        load_v.append(pltpu.make_async_copy(cv_hbm.at[rows], v_buf.at[rows], v_sem.at[g]))
        load_v[-1].start()
    load_wo = pltpu.make_async_copy(wo_hbm, wo_buf, load_sem.at[4])
    load_wo.start()

    column = lax.broadcasted_iota(jnp.int32, (1, D), 1)
    block = jnp.zeros((1, D), jnp.int32)
    for n in range(1, 8):
        block = block + (column >= n * FEATS).astype(jnp.int32)
    feature = column - block * FEATS
    feature_rows = lax.broadcasted_iota(jnp.int32, (FEATS, D), 0)
    spread_buf[...] = jnp.where(feature_rows == feature, 1.0, 0.0).astype(BF16)
    request = lax.broadcasted_iota(jnp.int32, (8, D), 0)
    masks = (
        (request == block) & (feature < HD),
        (request == block) & (feature >= HD),
    )

    load_tok.wait()
    pl.semaphore_wait(barrier, expected)

    def remote(src, dst, ssem, rsem, device):
        return pltpu.make_async_remote_copy(
            src_ref=src, dst_ref=dst, send_sem=ssem, recv_sem=rsem, device_id=device, device_id_type=MESH
        )

    tok_out = []
    for k in range(1, HEADS):
        copy = remote(
            tok_buf.at[me_head], tok_buf.at[me_head], tok_ssem.at[k], tok_rsem.at[k], head_peer(k)
        )
        copy.start()
        tok_out.append(copy)

    slots = (1 + core, 2 - core)
    own_shard = [
        remote(w_buf.at[core, 0], w_buf.at[core, slots[1 - n]], w_ssem.at[n], w_rsem.at[1 - n], z_peer(n))
        for n in range(2)
    ]
    passed_on = remote(w_buf.at[core, slots[0]], w_buf.at[core, 3], w_ssem.at[2], w_rsem.at[2], z_peer(1))

    def to_other_core(n):
        at = w_buf.at[core, (slots[0], slots[1], 3)[n]]
        return remote(at, at, pair_ssem.at[n], pair_rsem.at[n], other_core)

    for n in range(2):
        @pl.when(earlier[n])
        def _():
            pl.semaphore_signal(ready_sem.at[1 - n], inc=1, device_id=z_peer(n), device_id_type=MESH)

    @pl.when(twin_earlier)
    def _():
        for k in range(4, PEERS):
            pl.semaphore_signal(ready_sem.at[2], inc=1, device_id=near_peer(k), device_id_type=MESH)

    load_wu.wait()
    load_wd.wait()
    for n in range(2):
        @pl.when(jnp.logical_not(later[n]))
        def _():
            own_shard[n].start()

    for copy in tok_out:
        copy.wait_recv()
    for n in range(2):
        @pl.when(later[n])
        def _():
            pl.semaphore_wait(ready_sem.at[n], 1)
            own_shard[n].start()

    for n in range(HEADS):
        rows_buf[pl.ds(OWN * n, OWN), :] = tok_buf[n].astype(F32)
    for copy in smalls:
        copy.wait()
    normed = rms_scale(rows_buf[...], gain_attn_ref[...].reshape(1, D)).astype(BF16)

    for copy in loads:
        copy.wait()
    scale = scale_ref[...]
    scale = jnp.concatenate([scale, scale], axis=1)
    query = (times_rows(normed, wq_buf[...]) * scale).astype(BF16)
    new_key = times_rows(normed, wk_buf[...]).astype(BF16)
    new_value = times_rows(normed, wv_buf[...]).astype(BF16)
    spread_query = times(query, spread_buf[...])
    spread_value = times(new_value, spread_buf[...])
    product = query.astype(F32) * new_key.astype(F32)
    lane = lax.broadcasted_iota(jnp.int32, (ROWS, FEATS), 1)
    score_new = (
        jnp.sum(jnp.where(lane < HD, product, 0.0), axis=-1, keepdims=True),
        jnp.sum(jnp.where(lane >= HD, product, 0.0), axis=-1, keepdims=True),
    )
    eye = lax.broadcasted_iota(jnp.int32, (ROWS, ROWS), 0) == lax.broadcasted_iota(jnp.int32, (ROWS, ROWS), 1)
    lens = jnp.sum(jnp.where(eye, jnp.broadcast_to(lens_ref[...], (ROWS, ROWS)), 0), axis=-1, keepdims=True)

    slot = lax.broadcasted_iota(jnp.int32, (16, CACHE), 1)
    scores = []
    for g in range(4):
        at = slice(8 * g, 8 * g + 8)
        load_k[g].wait()
        left = jnp.concatenate([jnp.where(mask, spread_query[at], 0.0) for mask in masks], axis=0)
        scores.append(times(left.astype(BF16), k_buf[pl.ds(g * D, D), :]))
    own_shard[1].wait_recv()
    passed_on.start()
    to_other_core(0).start()
    own_shard[0].wait_recv()
    to_other_core(1).start()
    probs, prob_new, total = [], [], []
    for g in range(4):
        at = slice(8 * g, 8 * g + 8)
        fresh = jnp.concatenate([score_new[0][at], score_new[1][at]], axis=0)
        length = jnp.concatenate([lens[at], lens[at]], axis=0)
        valid = slot < length
        top = jnp.maximum(jnp.max(jnp.where(valid, scores[g], -jnp.inf), axis=-1, keepdims=True), fresh)
        weights = jnp.where(valid, jnp.exp(scores[g] - top), 0.0)
        weight_new = jnp.exp(fresh - top)
        total.append(jnp.sum(weights, axis=-1, keepdims=True) + weight_new)
        probs.append(weights.astype(BF16))
        prob_new.append(weight_new.astype(BF16).astype(F32))
    for g in range(4):
        at = slice(8 * g, 8 * g + 8)
        load_v[g].wait()
        summed = times_rows(probs[g], v_buf[pl.ds(g * D, D), :])
        picked = jnp.zeros((8, D), F32)
        for h in range(2):
            half = slice(8 * h, 8 * h + 8)
            result = (summed[half] + prob_new[g][half] * spread_value[at]) / total[g][half]
            picked = jnp.where(masks[h], result, picked)
        att_buf[pl.ds(8 * g, 8), :] = picked
    attended = times_rows(att_buf[...].astype(BF16), spread_buf[...]).astype(BF16)
    load_wo.wait()
    part = times(attended, wo_buf[...])
    for n in range(HEADS):
        part_send[n] = part[OWN * n : OWN * n + OWN].astype(BF16)
    part_out = []
    for k in range(1, HEADS):
        copy = remote(
            part_send.at[(me_head + k) % HEADS], part_recv.at[k], part_ssem.at[k], part_rsem.at[k], head_peer(k)
        )
        copy.start()
        part_out.append(copy)

    @pl.when(twin_later)
    def _():
        pl.semaphore_wait(ready_sem.at[2], 4)

    mid = tok_buf[me_head].astype(F32)
    mid = mid + part_send[me_head].astype(F32)
    for k, copy in enumerate(part_out, start=1):
        copy.wait_recv()
        mid = mid + part_recv[k].astype(F32)
    nm_buf[0] = rms_scale(mid, gain_mlp_ref[...].reshape(1, D)).astype(BF16)
    nm_out = []
    for k in range(1, PEERS):
        copy = remote(nm_buf.at[0], nm_buf.at[k], nm_ssem.at[k], nm_rsem.at[k], near_peer(k))
        copy.start()
        nm_out.append(copy)

    passed_on.wait_recv()
    to_other_core(2).start()
    for n in range(3):
        to_other_core(n).wait_recv()
    for copy in nm_out:
        copy.wait_recv()
    for n in range(PEERS):
        nm_rows[pl.ds(OWN * n, OWN), :] = nm_buf[n].astype(F32)
    normed_mid = nm_rows[...].astype(BF16)
    hidden = times_rows(normed_mid, w_buf[0].reshape(SHARDS * UNITS, D))
    hidden = (hidden / (1.0 + jnp.exp(-hidden))).astype(BF16)
    mixed = times(hidden, w_buf[1].reshape(SHARDS * UNITS, D))
    for n in range(PEERS):
        ff_send[n] = mixed[OWN * n : OWN * n + OWN].astype(BF16)
    ff_out = []
    for k in range(1, PEERS):
        copy = remote(ff_send.at[near_back(k)], ff_recv.at[k], ff_ssem.at[k], ff_rsem.at[k], near_peer(k))
        copy.start()
        ff_out.append(copy)
    result = mid + ff_send[0].astype(F32)
    for k, copy in enumerate(ff_out, start=1):
        copy.wait_recv()
        result = result + ff_recv[k].astype(F32)
    out_ref[...] = result.astype(BF16)

    for copy in tok_out + part_out + nm_out + ff_out:
        copy.wait_send()

    for copy in (*own_shard, passed_on, *(to_other_core(n) for n in range(3))):
        copy.wait_send()


def shards(
    tokens, norm_attn, query_scale, w_query, w_key, w_value, w_out, norm_mlp, w_up, w_down, cache_k, cache_v, lengths
):
    anywhere = pl.BlockSpec(memory_space=pl.ANY)
    dma = pltpu.SemaphoreType.DMA
    return pl.pallas_call(
        layer,
        out_shape=pltpu.VMEM((OWN, D), BF16),
        in_specs=[anywhere] * 13,
        out_specs=pl.BlockSpec(memory_space=pltpu.VMEM),
        scratch_shapes=[
            pltpu.VMEM((D,), F32),
            pltpu.VMEM((1, HD), F32),
            pltpu.VMEM((D,), F32),
            pltpu.VMEM((1, ROWS), jnp.int32),
            pltpu.VMEM((HEADS, OWN, D), BF16),
            pltpu.VMEM((ROWS, D), F32),
            pltpu.VMEM((FEATS, D), BF16),
            pltpu.VMEM((FEATS, D), BF16),
            pltpu.VMEM((FEATS, D), BF16),
            pltpu.VMEM((FEATS, D), BF16),
            pltpu.VMEM((ROWS * FEATS, CACHE), BF16),
            pltpu.VMEM((ROWS * FEATS, CACHE), BF16),
            pltpu.VMEM((2, SHARDS, UNITS, D), BF16),
            pltpu.VMEM((FEATS, D), BF16),
            pltpu.VMEM((ROWS, D), F32),
            pltpu.VMEM((HEADS, OWN, D), BF16),
            pltpu.VMEM((HEADS, OWN, D), BF16),
            pltpu.VMEM((PEERS, OWN, D), BF16),
            pltpu.VMEM((PEERS * OWN, D), F32),
            pltpu.VMEM((PEERS, OWN, D), BF16),
            pltpu.VMEM((PEERS, OWN, D), BF16),
            dma((7,)), dma((4,)), dma((4,)), dma((4,)), pltpu.SemaphoreType.REGULAR((3,)),
            dma((HEADS,)), dma((HEADS,)), dma((HEADS,)), dma((HEADS,)),
            dma((PEERS,)), dma((PEERS,)), dma((PEERS,)), dma((PEERS,)),
            dma((3,)), dma((3,)), dma((3,)), dma((3,)),
        ],
        compiler_params=pltpu.CompilerParams(
            collective_id=0, has_side_effects=True, vmem_limit_bytes=60 * 1024 * 1024
        ),
        name="decode_layer",
    )(
        tokens, norm_attn, query_scale.reshape(1, HD), w_query, w_key, w_value, w_out,
        norm_mlp, w_up, w_down, cache_k.reshape(ROWS * FEATS, CACHE),
        cache_v.reshape(ROWS * FEATS, CACHE), lengths.reshape(1, ROWS),
    )


def solution(mesh):
    in_specs = (
        P(("req", "head"), None),
        P(),
        P(),
        P("head", None),
        P("head", None),
        P("head", None),
        P("head", None),
        P(),
        P("req", None),
        P("req", None),
        P("req", "head", None),
        P("req", "head", None),
        P("req"),
    )
    out_specs = P(("req", "head"), None)
    return jax.shard_map(shards, mesh=mesh, in_specs=in_specs, out_specs=out_specs, check_vma=False)
```
